32 devices in a mesh: dp: 4 (over y, x), tm: 8 (over z, core).
Axes of the slice: x: 2, y: 2, z: 4, core: 2. Of those that a mesh axis runs over, the one named last changes fastest.
Arguments:
- wall_inputs: bfloat16 [4, 1024, 576], P('dp', 'tm'), may hold values from -6 to 6
- in_weight: bfloat16 [576, 1024], replicated, may hold values from -0.25 to 0.25
- tap_weights: bfloat16 [1, 2048, 1024], replicated, may hold values from -0.125 to 0.125
- out_weight: bfloat16 [1024, 576], replicated, may hold values from -0.1875 to 0.1875
- cotangent: bfloat16 [4, 1024, 576], P('dp', 'tm'), may hold values from -0.09375 to 0.09375
Outputs:
- prediction: float32 [4, 1024, 576], P('dp', 'tm')
- grad_in: float32 [576, 1024], replicated
- grad_taps: float32 [1, 2048, 1024], P(None, ('dp', 'tm'))
- grad_out: float32 [1024, 576], replicated
The draws below stay inside these ranges and needn't reach their ends.
All inputs are finite; a program needn't handle non-finite values.
Results may differ from the reference program's by a relative error of at most 0.0048.
Values may be sent and summed in bfloat16 or wider, within the bound.
A program may use at most 64 MiB of HBM per device.

```python
import jax
import jax.numpy as jnp
from jax import lax

C = 1024
IN = 576
OUT = 576
LAYERS = 1
DILATION = 512
MEMBERS = 4
TIME = 1024


def steps_of(key, dims, pieces, smallest, largest):
    def one(position, shards_of):
        heights = jax.random.uniform(jax.random.fold_in(jax.random.fold_in(key, 6), position), (shards_of,), jnp.float32, smallest / len(pieces), largest / len(pieces))
        return jnp.repeat(jnp.exp(heights), dims[position] // shards_of).reshape((-1,) + (1,) * (len(dims) - position - 1))

    level = one(*pieces[0])
    for cut in pieces[1:]:
        level = level * one(*cut)
    return level


def gaussian(stream_key, extent, deviation, limit, cuts=(), kind=jnp.bfloat16):
    factor_of = steps_of(stream_key, extent, cuts, -0.22, 0.18) if cuts else 1.0
    result = jax.random.normal(stream_key, extent, jnp.float32) * deviation * factor_of
    return jnp.minimum(jnp.maximum(result, -limit), limit).astype(kind)


def setup_inputs(seed: int = 0) -> dict:
    arg_keys = jax.random.split(jax.random.key(seed), 6)
    return {
        "wall_inputs": gaussian(arg_keys[0], (MEMBERS, TIME, IN), 1.0, 6.0, ((0, 4), (1, 8))),
        "in_weight": gaussian(arg_keys[1], (IN, C), IN ** -0.5, 0.25),
        "tap_weights": gaussian(arg_keys[2], (LAYERS, 2 * C, C), (2 * C) ** -0.5, 0.125),
        "out_weight": gaussian(arg_keys[3], (C, OUT), C ** -0.5, 0.1875),
        "cotangent": gaussian(arg_keys[4], (MEMBERS, TIME, OUT), (MEMBERS * TIME) ** -0.5, 0.09375, ((0, 4), (1, 8))),
    }


def lag_time(hidden, dilation):
    zeros = jnp.zeros((hidden.shape[0], dilation, hidden.shape[2]), hidden.dtype)
    return jnp.concatenate([zeros, hidden[:, :hidden.shape[1] - dilation]], axis=1)


def forward_time_offset(values, dilation):
    zeros = jnp.zeros((values.shape[0], dilation, values.shape[2]), values.dtype)
    return jnp.concatenate([values[:, dilation:], zeros], axis=1)


def project(left, weight):
    rows = left.reshape(-1, left.shape[-1])
    return jnp.dot(rows, weight, preferred_element_type=jnp.float32).reshape(left.shape[:-1] + (weight.shape[-1],))


def project_back(left, weight):
    rows = left.reshape(-1, left.shape[-1])
    step_outcome = lax.dot_general(rows, weight, (((1,), (1,)), ((), ())), preferred_element_type=jnp.float32)
    return step_outcome.reshape(left.shape[:-1] + (weight.shape[0],))


def contract_rows(left, right):
    return lax.dot_general(left.reshape(-1, left.shape[-1]), right.reshape(-1, right.shape[-1]),
                           (((0,), (0,)), ((), ())), preferred_element_type=jnp.float32)


def reference(wall_inputs, in_weight, tap_weights, out_weight, cotangent):
    hidden = project(wall_inputs, in_weight).astype(jnp.bfloat16)
    stored = []
    for layer_at in range(LAYERS):
        lagged = lag_time(hidden, DILATION)
        preact = project(lagged, tap_weights[layer_at, :C]) + project(hidden, tap_weights[layer_at, C:])
        activation_function = jnp.tanh(preact)
        stored.append((lagged, hidden, activation_function))
        hidden = (hidden.astype(jnp.float32) + activation_function).astype(jnp.bfloat16)
    prediction = project(hidden, out_weight)
    grad_out = contract_rows(hidden, cotangent)
    upstream = project_back(cotangent, out_weight)
    filter_tap_gradient = [None] * LAYERS
    for layer_at in reversed(range(LAYERS)):
        lagged, before, activation_function = stored[layer_at]
        pre_grad = (upstream * (1.0 - activation_function * activation_function)).astype(jnp.bfloat16)
        filter_tap_gradient[layer_at] = jnp.concatenate([contract_rows(lagged, pre_grad), contract_rows(before, pre_grad)], axis=0)
        direct = project_back(pre_grad, tap_weights[layer_at, C:])
        delayed = forward_time_offset(project_back(pre_grad, tap_weights[layer_at, :C]), DILATION)
        upstream = upstream + direct + delayed
    back_zero = upstream.astype(jnp.bfloat16)
    grad_in = contract_rows(wall_inputs, back_zero)
    return prediction, grad_in, jnp.stack(filter_tap_gradient), grad_out
```

```python
import jax
import jax.numpy as jnp
from jax import lax
from jax.experimental import pallas as pl
from jax.experimental.pallas import tpu as pltpu
from jax.sharding import PartitionSpec as P

LAYERS = 1
DILATION = 512


def from_behind(x, axis, by):
    size = lax.axis_size(axis)
    pairs = [(i, i + by) for i in range(size) if 0 <= i + by < size]
    return lax.ppermute(x, axis, pairs)


def project(left, weight):
    rows = left.reshape(-1, left.shape[-1])
    return jnp.dot(rows, weight, preferred_element_type=jnp.float32).reshape(
        left.shape[:-1] + (weight.shape[-1],)
    )


def project_back(left, weight):
    rows = left.reshape(-1, left.shape[-1])
    step_outcome = lax.dot_general(
        rows, weight, (((1,), (1,)), ((), ())), preferred_element_type=jnp.float32
    )
    return step_outcome.reshape(left.shape[:-1] + (weight.shape[0],))


def contract_rows(left, right):
    return lax.dot_general(
        left.reshape(-1, left.shape[-1]),
        right.reshape(-1, right.shape[-1]),
        (((0,), (0,)), ((), ())),
        preferred_element_type=jnp.float32,
    )


def lag_rows(hidden, dilation):
    shard_len = hidden.shape[1]
    whole_shards, remainder = divmod(dilation, shard_len)
    head_rows = hidden
    head_rows = from_behind(head_rows, "tm", whole_shards)
    return head_rows


def lead_sums(values, dilation):
    shard_len = values.shape[1]
    whole_shards, remainder = divmod(dilation, shard_len)
    head_rows = values
    head_rows = from_behind(head_rows.astype(jnp.bfloat16), "tm", -whole_shards).astype(
        head_rows.dtype
    )
    return head_rows


def reduce_taps(partial_value):
    per_member_split = lax.psum_scatter(partial_value, "dp", scatter_dimension=0, tiled=True)
    return lax.psum_scatter(per_member_split, "tm", scatter_dimension=0, tiled=True)


def on_device(wall_inputs, in_weight, tap_weights, out_weight, cotangent):
    channels = tap_weights.shape[2]
    hidden = project(wall_inputs, in_weight).astype(jnp.bfloat16)
    layer_at = 0
    lagged = lag_rows(hidden, DILATION)
    preact = project(lagged, tap_weights[layer_at, :channels]) + project(
        hidden, tap_weights[layer_at, channels:]
    )
    activation_function = jnp.tanh(preact)
    stored = [(lagged, hidden, activation_function)]
    hidden = (hidden.astype(jnp.float32) + activation_function).astype(jnp.bfloat16)
    prediction = project(hidden, out_weight)
    grad_out = lax.psum(contract_rows(hidden, cotangent), ("dp", "tm"))
    upstream = project_back(cotangent, out_weight)
    filter_tap_gradient = [None] * LAYERS
    for layer_at in reversed(range(LAYERS)):
        lagged, before, activation_function = stored[layer_at]
        pre_grad = (upstream * (1.0 - activation_function * activation_function)).astype(
            jnp.bfloat16
        )
        partial_value = jnp.concatenate(
            [contract_rows(lagged, pre_grad), contract_rows(before, pre_grad)], axis=0
        )
        filter_tap_gradient[layer_at] = reduce_taps(partial_value)
        direct = project_back(pre_grad, tap_weights[layer_at, channels:])
        delayed = lead_sums(project_back(pre_grad, tap_weights[layer_at, :channels]), DILATION)
        upstream = upstream + direct + delayed
    back_zero = upstream.astype(jnp.bfloat16)
    grad_in = lax.psum(contract_rows(wall_inputs, back_zero), ("dp", "tm"))
    return (prediction, grad_in, jnp.stack(filter_tap_gradient), grad_out)


BF16 = jnp.bfloat16
F32 = jnp.float32


def reduce_kernel(
    t_ref, i_ref, o_ref, p_ref,
    t_out, i_out, o_out, p_out,
    t_r1, i_r1, o_r1, t_s2, i_s2, o_s2, t_r2, i_r2, o_r2,
    t_z, i_z, o_z, t_rz, i_rz, o_rz, t_fin,
    send_sems, recv_sems,
):
    me = lax.axis_index("dp")
    tm = lax.axis_index("tm")
    z, core = tm // 2, tm % 2
    x_peer = me + 1 - 2 * (me % 2)
    y_peer = me + 2 - 4 * (me // 2)
    n1 = x_peer * (1 - core) + y_peer * core
    n2 = y_peer * (1 - core) + x_peer * core
    far = 3 - me
    others = [z + 1 - 2 * (z % 2), (z + 2) % 4, 3 - z]
    twin = z * 2 + 1 - core

    to_n1 = {"dp": n1, "tm": tm}
    to_n2 = {"dp": n2, "tm": tm}
    to_z = [{"dp": me, "tm": other * 2 + core} for other in others]
    to_twin = {"dp": me, "tm": twin}

    barrier = pltpu.get_barrier_semaphore()
    peers = [to_n1, to_n2, to_twin] + to_z
    for peer in peers:
        pl.semaphore_signal(barrier, inc=1, device_id=peer, device_id_type=pl.DeviceIdType.MESH)
    pl.semaphore_wait(barrier, len(peers))

    made = []

    def send(src, dst, peer):
        at = len(made)
        copy = pltpu.make_async_remote_copy(
            src_ref=src, dst_ref=dst, send_sem=send_sems.at[at], recv_sem=recv_sems.at[at],
            device_id=peer, device_id_type=pl.DeviceIdType.MESH,
        )
        copy.start()
        made.append(copy)
        return copy

    def arrived(copies):
        for copy in copies:
            copy.wait_recv()

    def over(count, body):
        def step(at, carry):
            body(at)
            return carry

        lax.fori_loop(0, count, step, 0)

    io1 = (i_ref, i_r1, i_s2, i_r2, i_z, i_rz)
    oo1 = (o_ref, o_r1, o_s2, o_r2, o_z, o_rz)
    tt1 = (t_ref, t_r1, t_s2, t_r2, t_z, t_rz)

    def first_hop(pack, block, slot):
        return send(pack[0].at[block], pack[1].at[slot], to_n1)

    def second_hop(pack):
        local, r1, s2, r2 = pack[:4]

        def body(at):
            s2[at] = (local[n2, at].astype(F32) + r1[0, at].astype(F32)).astype(BF16)

        over(4, body)
        return send(s2, r2, to_n2)

    def plane_sum(pack, at):
        local, r1, _, r2 = pack[:4]
        return local[me, at].astype(F32) + r1[1, at].astype(F32) + r2[at].astype(F32)

    def z_hop(pack):
        out, landing = pack[4], pack[5]

        def body(at):
            out[at] = plane_sum(pack, at).astype(BF16)

        over(4, body)
        return [
            send(out.at[other], landing.at[k], to_z[k]) for k, other in enumerate(others)
        ]

    def z_sum(pack):
        landing = pack[5]
        total = plane_sum(pack, z)
        for k in range(3):
            total = total + landing[k].astype(F32)
        return total

    i_a = first_hop(io1, far, 0)
    o_a = first_hop(oo1, far, 0)
    i_b = first_hop(io1, n1, 1)
    o_b = first_hop(oo1, n1, 1)
    t_a = first_hop(tt1, far, 0)
    t_b = first_hop(tt1, n1, 1)
    p_copy = send(p_ref, p_out, to_z[1])

    arrived([i_a])
    i_2 = second_hop(io1)
    arrived([o_a])
    o_2 = second_hop(oo1)
    arrived([i_b, i_2])
    i_zs = z_hop(io1)
    arrived([o_b, o_2])
    o_zs = z_hop(oo1)
    arrived([t_a])
    t_2 = second_hop(tt1)

    arrived(i_zs)
    i_out[core, me, z] = z_sum(io1).astype(BF16)
    i_mine = i_out.at[core, me, z]
    i_ag = [send(i_mine, i_mine, peer) for peer in to_z]
    arrived(o_zs)
    o_out[core, me, z] = z_sum(oo1).astype(BF16)
    o_mine = o_out.at[core, me, z]
    o_ag = [send(o_mine, o_mine, peer) for peer in to_z]

    def forward(block, peer):
        return [
            send(i_out.at[core, block], i_out.at[core, block], peer),
            send(o_out.at[core, block], o_out.at[core, block], peer),
        ]

    arrived(i_ag + o_ag)
    hop1 = forward(me, to_n1)
    hop2 = forward(me, to_n2)
    twin_me = forward(me, to_twin)
    arrived([t_b, t_2])
    t_zs = z_hop(tt1)

    arrived(hop1)
    hop3 = forward(n1, to_n2)
    twin_n1 = forward(n1, to_twin)
    arrived(hop2)
    twin_n2 = forward(n2, to_twin)

    arrived(t_zs)
    total = z_sum(tt1)
    t_fin[0] = total[:64]
    t_fin[1] = total[64:]
    t_twin = send(t_fin.at[1 - core], t_out.at[core], to_twin)
    t_out[core] = t_fin[core]

    arrived(hop3)
    twin_far = forward(far, to_twin)
    arrived([t_twin, p_copy] + twin_me + twin_n1 + twin_n2 + twin_far)
    for copy in made:
        copy.wait_send()


def reduce_all(taps, inner, outer, pred):
    vmem = pl.BlockSpec(memory_space=pltpu.VMEM)
    t_blk, i_blk, o_blk = taps.shape[2:], inner.shape[2:], outer.shape[2:]
    blocks = (t_blk, i_blk, o_blk)
    scratch = []
    for lead in ((2, 4), (4,), (4,), (4,), (3,)):
        scratch += [pltpu.VMEM(lead + blk, BF16) for blk in blocks]
    scratch += [
        pltpu.VMEM((2, t_blk[0] // 2, t_blk[1]), F32),
        pltpu.SemaphoreType.DMA((41,)),
        pltpu.SemaphoreType.DMA((41,)),
    ]
    return pl.pallas_call(
        reduce_kernel,
        out_shape=(
            jax.ShapeDtypeStruct((2, t_blk[0] // 2, t_blk[1]), F32),
            jax.ShapeDtypeStruct((2, 4, 4) + i_blk, BF16),
            jax.ShapeDtypeStruct((2, 4, 4) + o_blk, BF16),
            jax.ShapeDtypeStruct(pred.shape, F32),
        ),
        in_specs=[vmem] * 4,
        out_specs=[vmem] * 4,
        scratch_shapes=scratch,
        compiler_params=pltpu.CompilerParams(
            collective_id=0, has_side_effects=True, vmem_limit_bytes=48 * 1024 * 1024
        ),
    )(taps, inner, outer, pred)


def on_small_slice(wall_inputs, in_weight, tap_weights, out_weight, cotangent):
    channels = tap_weights.shape[2]
    wide = channels // 2
    rows, features = wall_inputs.shape[1:]
    half = rows // 2
    tm = lax.axis_index("tm")
    shards = lax.axis_size("tm")
    early = tm < shards // 2
    core = tm % 2
    delayed_w, current_w = tap_weights[0, :channels], tap_weights[0, channels:]

    local = jnp.stack([wall_inputs[0], cotangent[0]])
    keep = jnp.where(early, local[:, :half], local[:, half:])
    give = jnp.where(early, local[:, half:], local[:, :half])
    got = lax.ppermute(give, "tm", [(i, (i + shards // 2) % shards) for i in range(shards)])
    low, high = jnp.where(early, keep, got), jnp.where(early, got, keep)
    pairs = jnp.stack([low, high])
    twin = lax.ppermute(pairs, "tm", [(i, i + 1 - 2 * (i % 2)) for i in range(shards)])
    everything = jnp.stack([pairs, twin], axis=1)
    inputs = everything[:, :, 0].reshape(4 * half, features)
    cots = everything[:, :, 1].reshape(4 * half, features)

    hidden = project(inputs, in_weight).astype(BF16)
    lag = hidden[: 2 * half]
    from_lag = project(lag, delayed_w)
    preact = project(hidden, current_w) + jnp.concatenate([jnp.zeros_like(from_lag), from_lag])
    squash = jnp.tanh(preact)
    hidden_1 = (hidden.astype(F32) + squash).astype(BF16)
    own = jnp.concatenate([hidden_1[:half], hidden_1[2 * half : 3 * half]])
    pred = project(own, out_weight)
    upstream = project_back(cots, out_weight)
    pre_grad = (upstream * (1.0 - squash * squash)).astype(BF16)
    late = pre_grad[2 * half :]
    from_late = project_back(late, delayed_w)
    back = upstream + project_back(pre_grad, current_w) + jnp.concatenate(
        [from_late, jnp.zeros_like(from_late)]
    )
    back = back.astype(BF16)

    pre_cols = lax.dynamic_slice_in_dim(pre_grad, core * wide, wide, 1)
    back_cols = lax.dynamic_slice_in_dim(back, core * wide, wide, 1)
    hidden_cols = lax.dynamic_slice_in_dim(hidden_1, core * wide, wide, 1)
    taps = jnp.concatenate(
        [contract_rows(lag, pre_cols[2 * half :]), contract_rows(hidden, pre_cols)], axis=0
    ).astype(BF16).reshape(4, 4, channels // 8, wide)
    inner = contract_rows(inputs, back_cols).astype(BF16)
    inner = inner.reshape(4, features // 4, 4, wide // 4).transpose(0, 2, 1, 3)
    outer = contract_rows(hidden_cols, cots).astype(BF16).reshape(4, 4, wide // 16, features)

    pred_keep = jnp.where(early, pred[:half], pred[half:])
    pred_give = jnp.where(early, pred[half:], pred[:half])
    t_sum, i_sum, o_sum, pred_got = reduce_all(taps, inner, outer, pred_give)
    prediction = jnp.concatenate(
        [jnp.where(early, pred_keep, pred_got), jnp.where(early, pred_got, pred_keep)]
    )[None]
    grad_taps = t_sum.transpose(1, 0, 2).reshape(1, channels // 16, channels)
    grad_in = i_sum.transpose(1, 3, 0, 2, 4).reshape(features, channels).astype(F32)
    grad_out = o_sum.reshape(channels, features).astype(F32)
    return prediction, grad_in, grad_taps, grad_out


def solution(mesh):
    in_specs = (P("dp", "tm", None), P(), P(), P(), P("dp", "tm", None))
    out_specs = (P("dp", "tm", None), P(), P(None, ("dp", "tm"), None), P())
    small = mesh.shape["dp"] == 4 and mesh.shape["tm"] == 8
    return jax.shard_map(
        on_small_slice if small else on_device,
        mesh=mesh, in_specs=in_specs, out_specs=out_specs, check_vma=False,
    )
```

```python
import jax
import jax.numpy as jnp
from jax import lax
from jax.experimental import pallas as pl
from jax.experimental.pallas import tpu as pltpu
from jax.sharding import PartitionSpec as P

LAYERS = 1
DILATION = 512


def from_behind(x, axis, by):
    size = lax.axis_size(axis)
    pairs = [(i, i + by) for i in range(size) if 0 <= i + by < size]
    return lax.ppermute(x, axis, pairs)


def project(left, weight):
    rows = left.reshape(-1, left.shape[-1])
    return jnp.dot(rows, weight, preferred_element_type=jnp.float32).reshape(
        left.shape[:-1] + (weight.shape[-1],)
    )


def project_back(left, weight):
    rows = left.reshape(-1, left.shape[-1])
    step_outcome = lax.dot_general(
        rows, weight, (((1,), (1,)), ((), ())), preferred_element_type=jnp.float32
    )
    return step_outcome.reshape(left.shape[:-1] + (weight.shape[0],))


def contract_rows(left, right):
    return lax.dot_general(
        left.reshape(-1, left.shape[-1]),
        right.reshape(-1, right.shape[-1]),
        (((0,), (0,)), ((), ())),
        preferred_element_type=jnp.float32,
    )


def lag_rows(hidden, dilation):
    shard_len = hidden.shape[1]
    whole_shards, remainder = divmod(dilation, shard_len)
    head_rows = hidden
    head_rows = from_behind(head_rows, "tm", whole_shards)
    return head_rows


def lead_sums(values, dilation):
    shard_len = values.shape[1]
    whole_shards, remainder = divmod(dilation, shard_len)
    head_rows = values
    head_rows = from_behind(head_rows.astype(jnp.bfloat16), "tm", -whole_shards).astype(
        head_rows.dtype
    )
    return head_rows


def reduce_taps(partial_value):
    per_member_split = lax.psum_scatter(partial_value, "dp", scatter_dimension=0, tiled=True)
    return lax.psum_scatter(per_member_split, "tm", scatter_dimension=0, tiled=True)


def on_device(wall_inputs, in_weight, tap_weights, out_weight, cotangent):
    channels = tap_weights.shape[2]
    hidden = project(wall_inputs, in_weight).astype(jnp.bfloat16)
    layer_at = 0
    lagged = lag_rows(hidden, DILATION)
    preact = project(lagged, tap_weights[layer_at, :channels]) + project(
        hidden, tap_weights[layer_at, channels:]
    )
    activation_function = jnp.tanh(preact)
    stored = [(lagged, hidden, activation_function)]
    hidden = (hidden.astype(jnp.float32) + activation_function).astype(jnp.bfloat16)
    prediction = project(hidden, out_weight)
    grad_out = lax.psum(contract_rows(hidden, cotangent), ("dp", "tm"))
    upstream = project_back(cotangent, out_weight)
    filter_tap_gradient = [None] * LAYERS
    for layer_at in reversed(range(LAYERS)):
        lagged, before, activation_function = stored[layer_at]
        pre_grad = (upstream * (1.0 - activation_function * activation_function)).astype(
            jnp.bfloat16
        )
        partial_value = jnp.concatenate(
            [contract_rows(lagged, pre_grad), contract_rows(before, pre_grad)], axis=0
        )
        filter_tap_gradient[layer_at] = reduce_taps(partial_value)
        direct = project_back(pre_grad, tap_weights[layer_at, channels:])
        delayed = lead_sums(project_back(pre_grad, tap_weights[layer_at, :channels]), DILATION)
        upstream = upstream + direct + delayed
    back_zero = upstream.astype(jnp.bfloat16)
    grad_in = lax.psum(contract_rows(wall_inputs, back_zero), ("dp", "tm"))
    return (prediction, grad_in, jnp.stack(filter_tap_gradient), grad_out)


BF16 = jnp.bfloat16
F32 = jnp.float32


def reduce_kernel(
    t_ref, i_ref, o_ref, p_ref,
    t_out, i_out, o_out, p_out,
    t_r1, i_r1, o_r1, t_s2, i_s2, o_s2, t_r2, i_r2, o_r2,
    t_z, i_z, o_z, t_rz, i_rz, o_rz, t_fin,
    send_sems, recv_sems,
):
    me = lax.axis_index("dp")
    tm = lax.axis_index("tm")
    z, core = tm // 2, tm % 2
    x_peer = me + 1 - 2 * (me % 2)
    y_peer = me + 2 - 4 * (me // 2)
    n1 = x_peer * (1 - core) + y_peer * core
    n2 = y_peer * (1 - core) + x_peer * core
    far = 3 - me
    others = [z + 1 - 2 * (z % 2), (z + 2) % 4, 3 - z]
    twin = z * 2 + 1 - core

    to_n1 = {"dp": n1, "tm": tm}
    to_n2 = {"dp": n2, "tm": tm}
    to_z = [{"dp": me, "tm": other * 2 + core} for other in others]
    to_twin = {"dp": me, "tm": twin}

    barrier = pltpu.get_barrier_semaphore()
    peers = [to_n1, to_n2, to_twin] + to_z
    for peer in peers:
        pl.semaphore_signal(barrier, inc=1, device_id=peer, device_id_type=pl.DeviceIdType.MESH)
    pl.semaphore_wait(barrier, len(peers))

    made = []

    def send(src, dst, peer):
        at = len(made)
        copy = pltpu.make_async_remote_copy(
            src_ref=src, dst_ref=dst, send_sem=send_sems.at[at], recv_sem=recv_sems.at[at],
            device_id=peer, device_id_type=pl.DeviceIdType.MESH,
        )
        copy.start()
        made.append(copy)
        return copy

    def arrived(copies):
        for copy in copies:
            copy.wait_recv()

    def over(count, body):
        def step(at, carry):
            body(at)
            return carry

        lax.fori_loop(0, count, step, 0)

    io1 = (i_ref, i_r1, i_s2, i_r2, i_z, i_rz)
    oo1 = (o_ref, o_r1, o_s2, o_r2, o_z, o_rz)
    tt1 = (t_ref, t_r1, t_s2, t_r2, t_z, t_rz)
    tall = i_s2.shape[0]
    lanes = i_rz.shape[2]

    def rows_of(block):
        return pl.ds(pl.multiple_of(block * tall, 16), tall)

    def cols_of(at):
        return pl.ds(pl.multiple_of(at * lanes, 128), lanes)

    def first_hop(pack, block, slot):
        flat = len(pack[0].shape) == 2
        src = pack[0].at[rows_of(block)] if flat else pack[0].at[block]
        return send(src, pack[1].at[slot], to_n1)

    def second_hop(pack):
        local, r1, s2, r2 = pack[:4]

        def body(at):
            if len(local.shape) == 2:
                cut = cols_of(at)
                mine = local[rows_of(n2), cut].astype(F32)
                s2[:, cut] = (mine + r1[0, :, cut].astype(F32)).astype(BF16)
            else:
                s2[at] = (local[n2, at].astype(F32) + r1[0, at].astype(F32)).astype(BF16)

        over(4, body)
        return send(s2, r2, to_n2)

    def plane_sum(pack, at):
        local, r1, _, r2 = pack[:4]
        if len(local.shape) == 2:
            cut = cols_of(at)
            mine, first, second = local[rows_of(me), cut], r1[1, :, cut], r2[:, cut]
        else:
            mine, first, second = local[me, at], r1[1, at], r2[at]
        return mine.astype(F32) + first.astype(F32) + second.astype(F32)

    def z_hop(pack):
        out, landing = pack[4], pack[5]
        flat = len(out.shape) == 2

        def body(at):
            value = plane_sum(pack, at).astype(BF16)
            if flat:
                out[:, cols_of(at)] = value
            else:
                out[at] = value

        over(4, body)
        return [
            send(out.at[:, cols_of(other)] if flat else out.at[other], landing.at[k], to_z[k])
            for k, other in enumerate(others)
        ]

    def z_sum(pack):
        landing = pack[5]
        total = plane_sum(pack, z)
        for k in range(3):
            total = total + landing[k].astype(F32)
        return total

    i_a = first_hop(io1, far, 0)
    o_a = first_hop(oo1, far, 0)
    i_b = first_hop(io1, n1, 1)
    o_b = first_hop(oo1, n1, 1)
    t_a = first_hop(tt1, far, 0)
    t_b = first_hop(tt1, n1, 1)
    p_copy = send(p_ref, p_out, to_z[1])

    arrived([i_a])
    i_2 = second_hop(io1)
    arrived([o_a])
    o_2 = second_hop(oo1)
    arrived([i_b, i_2])
    i_zs = z_hop(io1)
    arrived([o_b, o_2])
    o_zs = z_hop(oo1)
    arrived([t_a])
    t_2 = second_hop(tt1)

    arrived(i_zs)
    i_mine = i_out.at[rows_of(me), cols_of(core * 4 + z)]
    i_out[rows_of(me), cols_of(core * 4 + z)] = z_sum(io1).astype(BF16)
    i_ag = [send(i_mine, i_mine, peer) for peer in to_z]
    arrived(o_zs)
    o_mine = o_out.at[rows_of(me), cols_of(core * 4 + z)]
    o_out[rows_of(me), cols_of(core * 4 + z)] = z_sum(oo1).astype(BF16)
    o_ag = [send(o_mine, o_mine, peer) for peer in to_z]

    def forward(block, peer):
        wide = pl.ds(pl.multiple_of(core * 4 * lanes, 128), 4 * lanes)
        i_part = i_out.at[rows_of(block), wide]
        o_part = o_out.at[rows_of(block), wide]
        return [send(i_part, i_part, peer), send(o_part, o_part, peer)]

    arrived(i_ag + o_ag)
    hop1 = forward(me, to_n1)
    hop2 = forward(me, to_n2)
    twin_me = forward(me, to_twin)
    arrived([t_b, t_2])
    t_zs = z_hop(tt1)

    arrived(hop1)
    hop3 = forward(n1, to_n2)
    twin_n1 = forward(n1, to_twin)
    arrived(hop2)
    twin_n2 = forward(n2, to_twin)

    arrived(t_zs)
    total = z_sum(tt1)
    t_fin[0] = total[:64]
    t_fin[1] = total[64:]
    t_twin = send(t_fin.at[1 - core], t_out.at[core], to_twin)
    t_out[core] = t_fin[core]

    arrived(hop3)
    twin_far = forward(far, to_twin)
    arrived([t_twin, p_copy] + twin_me + twin_n1 + twin_n2 + twin_far)
    for copy in made:
        copy.wait_send()


def reduce_all(taps, inner, outer, pred):
    vmem = pl.BlockSpec(memory_space=pltpu.VMEM)
    t_blk = taps.shape[2:]
    features, wide = inner.shape
    tall, lanes = features // 4, wide // 4
    scratch = []
    for lead in ((2,), (), (), ()):
        flat = pltpu.VMEM(lead + (tall, wide), BF16)
        scratch += [pltpu.VMEM(lead + (4,) + t_blk, BF16), flat, flat]
    landing = pltpu.VMEM((3, tall, lanes), BF16)
    scratch += [pltpu.VMEM((3,) + t_blk, BF16), landing, landing]
    scratch += [
        pltpu.VMEM((2, t_blk[0] // 2, t_blk[1]), F32),
        pltpu.SemaphoreType.DMA((41,)),
        pltpu.SemaphoreType.DMA((41,)),
    ]
    return pl.pallas_call(
        reduce_kernel,
        out_shape=(
            jax.ShapeDtypeStruct((2, t_blk[0] // 2, t_blk[1]), F32),
            jax.ShapeDtypeStruct((features, 2 * wide), BF16),
            jax.ShapeDtypeStruct((features, 2 * wide), BF16),
            jax.ShapeDtypeStruct(pred.shape, F32),
        ),
        in_specs=[vmem] * 4,
        out_specs=[vmem] * 4,
        scratch_shapes=scratch,
        compiler_params=pltpu.CompilerParams(
            collective_id=0, has_side_effects=True, vmem_limit_bytes=24 * 1024 * 1024
        ),
    )(taps, inner, outer, pred)


def on_small_slice(wall_inputs, in_weight, tap_weights, out_weight, cotangent):
    channels = tap_weights.shape[2]
    wide = channels // 2
    rows, features = wall_inputs.shape[1:]
    half = rows // 2
    tm = lax.axis_index("tm")
    shards = lax.axis_size("tm")
    early = tm < shards // 2
    core = tm % 2
    delayed_w, current_w = tap_weights[0, :channels], tap_weights[0, channels:]

    local = jnp.stack([wall_inputs[0], cotangent[0]])
    keep = jnp.where(early, local[:, :half], local[:, half:])
    give = jnp.where(early, local[:, half:], local[:, :half])
    got = lax.ppermute(give, "tm", [(i, (i + shards // 2) % shards) for i in range(shards)])
    low, high = jnp.where(early, keep, got), jnp.where(early, got, keep)
    pairs = jnp.stack([low, high])
    twin = lax.ppermute(pairs, "tm", [(i, i + 1 - 2 * (i % 2)) for i in range(shards)])
    everything = jnp.stack([pairs, twin], axis=1)
    inputs = everything[:, :, 0].reshape(4 * half, features)
    cots = everything[:, :, 1].reshape(4 * half, features)

    hidden = project(inputs, in_weight).astype(BF16)
    lag = hidden[: 2 * half]
    from_lag = project(lag, delayed_w)
    preact = project(hidden, current_w) + jnp.concatenate([jnp.zeros_like(from_lag), from_lag])
    squash = jnp.tanh(preact)
    hidden_1 = (hidden.astype(F32) + squash).astype(BF16)
    own = jnp.concatenate([hidden_1[:half], hidden_1[2 * half : 3 * half]])
    pred = project(own, out_weight)
    upstream = project_back(cots, out_weight)
    pre_grad = (upstream * (1.0 - squash * squash)).astype(BF16)
    late = pre_grad[2 * half :]
    from_late = project_back(late, delayed_w)
    back = upstream + project_back(pre_grad, current_w) + jnp.concatenate(
        [from_late, jnp.zeros_like(from_late)]
    )
    back = back.astype(BF16)

    pre_cols = lax.dynamic_slice_in_dim(pre_grad, core * wide, wide, 1)
    back_cols = lax.dynamic_slice_in_dim(back, core * wide, wide, 1)
    hidden_cols = lax.dynamic_slice_in_dim(hidden_1, core * wide, wide, 1)
    lagged = jnp.concatenate([jnp.zeros_like(lag), lag])
    both = jnp.concatenate([lagged, hidden], axis=1)
    taps = contract_rows(both, pre_cols).astype(BF16).reshape(4, 4, channels // 8, wide)
    inner = contract_rows(inputs, back_cols).astype(BF16)
    outer = contract_rows(cots, hidden_cols).astype(BF16)

    pred_keep = jnp.where(early, pred[:half], pred[half:])
    pred_give = jnp.where(early, pred[half:], pred[:half])
    t_sum, i_sum, o_sum, pred_got = reduce_all(taps, inner, outer, pred_give)
    prediction = jnp.concatenate(
        [jnp.where(early, pred_keep, pred_got), jnp.where(early, pred_got, pred_keep)]
    )[None]
    grad_taps = t_sum.transpose(1, 0, 2).reshape(1, channels // 16, channels)
    grad_in = i_sum.astype(F32)
    grad_out = o_sum.astype(F32).T
    return prediction, grad_in, grad_taps, grad_out


def solution(mesh):
    in_specs = (P("dp", "tm", None), P(), P(), P(), P("dp", "tm", None))
    out_specs = (P("dp", "tm", None), P(), P(None, ("dp", "tm"), None), P())
    small = mesh.shape["dp"] == 4 and mesh.shape["tm"] == 8
    return jax.shard_map(
        on_small_slice if small else on_device,
        mesh=mesh, in_specs=in_specs, out_specs=out_specs, check_vma=False,
    )
```

```python
import jax
import jax.numpy as jnp
from jax import lax
from jax.experimental import pallas as pl
from jax.experimental.pallas import tpu as pltpu
from jax.sharding import PartitionSpec as P

LAYERS = 1
DILATION = 512


def from_behind(x, axis, by):
    size = lax.axis_size(axis)
    pairs = [(i, i + by) for i in range(size) if 0 <= i + by < size]
    return lax.ppermute(x, axis, pairs)


def project(left, weight):
    rows = left.reshape(-1, left.shape[-1])
    return jnp.dot(rows, weight, preferred_element_type=jnp.float32).reshape(
        left.shape[:-1] + (weight.shape[-1],)
    )


def project_back(left, weight):
    rows = left.reshape(-1, left.shape[-1])
    step_outcome = lax.dot_general(
        rows, weight, (((1,), (1,)), ((), ())), preferred_element_type=jnp.float32
    )
    return step_outcome.reshape(left.shape[:-1] + (weight.shape[0],))


def contract_rows(left, right):
    return lax.dot_general(
        left.reshape(-1, left.shape[-1]),
        right.reshape(-1, right.shape[-1]),
        (((0,), (0,)), ((), ())),
        preferred_element_type=jnp.float32,
    )


def lag_rows(hidden, dilation):
    shard_len = hidden.shape[1]
    whole_shards, remainder = divmod(dilation, shard_len)
    head_rows = hidden
    head_rows = from_behind(head_rows, "tm", whole_shards)
    return head_rows


def lead_sums(values, dilation):
    shard_len = values.shape[1]
    whole_shards, remainder = divmod(dilation, shard_len)
    head_rows = values
    head_rows = from_behind(head_rows.astype(jnp.bfloat16), "tm", -whole_shards).astype(
        head_rows.dtype
    )
    return head_rows


def reduce_taps(partial_value):
    per_member_split = lax.psum_scatter(partial_value, "dp", scatter_dimension=0, tiled=True)
    return lax.psum_scatter(per_member_split, "tm", scatter_dimension=0, tiled=True)


def on_device(wall_inputs, in_weight, tap_weights, out_weight, cotangent):
    channels = tap_weights.shape[2]
    hidden = project(wall_inputs, in_weight).astype(jnp.bfloat16)
    layer_at = 0
    lagged = lag_rows(hidden, DILATION)
    preact = project(lagged, tap_weights[layer_at, :channels]) + project(
        hidden, tap_weights[layer_at, channels:]
    )
    activation_function = jnp.tanh(preact)
    stored = [(lagged, hidden, activation_function)]
    hidden = (hidden.astype(jnp.float32) + activation_function).astype(jnp.bfloat16)
    prediction = project(hidden, out_weight)
    grad_out = lax.psum(contract_rows(hidden, cotangent), ("dp", "tm"))
    upstream = project_back(cotangent, out_weight)
    filter_tap_gradient = [None] * LAYERS
    for layer_at in reversed(range(LAYERS)):
        lagged, before, activation_function = stored[layer_at]
        pre_grad = (upstream * (1.0 - activation_function * activation_function)).astype(
            jnp.bfloat16
        )
        partial_value = jnp.concatenate(
            [contract_rows(lagged, pre_grad), contract_rows(before, pre_grad)], axis=0
        )
        filter_tap_gradient[layer_at] = reduce_taps(partial_value)
        direct = project_back(pre_grad, tap_weights[layer_at, channels:])
        delayed = lead_sums(project_back(pre_grad, tap_weights[layer_at, :channels]), DILATION)
        upstream = upstream + direct + delayed
    back_zero = upstream.astype(jnp.bfloat16)
    grad_in = lax.psum(contract_rows(wall_inputs, back_zero), ("dp", "tm"))
    return (prediction, grad_in, jnp.stack(filter_tap_gradient), grad_out)


BF16 = jnp.bfloat16
F32 = jnp.float32


def reduce_kernel(
    t_ref, u_ref, i_ref, o_ref, p_ref,
    t_out, i_out, o_out, p_out,
    t_r1, u_r1, i_r1, o_r1, t_s2, u_s2, i_s2, o_s2, t_r2, u_r2, i_r2, o_r2,
    t_z, u_z, i_z, o_z, t_rz, u_rz, i_rz, o_rz, t_fin, u_fin,
    send_sems, recv_sems,
):
    me = lax.axis_index("dp")
    tm = lax.axis_index("tm")
    z, core = tm // 2, tm % 2
    x_peer = me + 1 - 2 * (me % 2)
    y_peer = me + 2 - 4 * (me // 2)
    n1 = x_peer * (1 - core) + y_peer * core
    n2 = y_peer * (1 - core) + x_peer * core
    far = 3 - me
    others = [z + 1 - 2 * (z % 2), (z + 2) % 4, 3 - z]
    twin = z * 2 + 1 - core

    to_n1 = {"dp": n1, "tm": tm}
    to_n2 = {"dp": n2, "tm": tm}
    to_z = [{"dp": me, "tm": other * 2 + core} for other in others]
    to_twin = {"dp": me, "tm": twin}

    barrier = pltpu.get_barrier_semaphore()
    peers = [to_n1, to_n2, to_twin] + to_z
    for peer in peers:
        pl.semaphore_signal(barrier, inc=1, device_id=peer, device_id_type=pl.DeviceIdType.MESH)
    pl.semaphore_wait(barrier, len(peers))

    made = []

    def send(src, dst, peer):
        at = len(made)
        copy = pltpu.make_async_remote_copy(
            src_ref=src, dst_ref=dst, send_sem=send_sems.at[at], recv_sem=recv_sems.at[at],
            device_id=peer, device_id_type=pl.DeviceIdType.MESH,
        )
        copy.start()
        made.append(copy)
        return copy

    def arrived(copies):
        for copy in copies:
            copy.wait_recv()

    def over(count, body):
        def step(at, carry):
            body(at)
            return carry

        lax.fori_loop(0, count, step, 0)

    io1 = (i_ref, i_r1, i_s2, i_r2, i_z, i_rz)
    oo1 = (o_ref, o_r1, o_s2, o_r2, o_z, o_rz)
    tt1 = (t_ref, t_r1, t_s2, t_r2, t_z, t_rz)
    uu1 = (u_ref, u_r1, u_s2, u_r2, u_z, u_rz)
    tall = i_s2.shape[0]
    lanes = i_rz.shape[2]

    def rows_of(block):
        return pl.ds(pl.multiple_of(block * tall, 16), tall)

    def cols_of(at):
        return pl.ds(pl.multiple_of(at * lanes, 128), lanes)

    def first_hop(pack, block, slot):
        flat = len(pack[0].shape) == 2
        src = pack[0].at[rows_of(block)] if flat else pack[0].at[block]
        return send(src, pack[1].at[slot], to_n1)

    def second_hop(pack):
        local, r1, s2, r2 = pack[:4]

        def body(at):
            if len(local.shape) == 2:
                cut = cols_of(at)
                mine = local[rows_of(n2), cut].astype(F32)
                s2[:, cut] = (mine + r1[0, :, cut].astype(F32)).astype(BF16)
            else:
                s2[at] = (local[n2, at].astype(F32) + r1[0, at].astype(F32)).astype(BF16)

        over(4, body)
        return send(s2, r2, to_n2)

    def plane_sum(pack, at):
        local, r1, _, r2 = pack[:4]
        if len(local.shape) == 2:
            cut = cols_of(at)
            mine, first, second = local[rows_of(me), cut], r1[1, :, cut], r2[:, cut]
        else:
            mine, first, second = local[me, at], r1[1, at], r2[at]
        return mine.astype(F32) + first.astype(F32) + second.astype(F32)

    def z_hop(pack):
        out, landing = pack[4], pack[5]
        flat = len(out.shape) == 2

        def body(at):
            value = plane_sum(pack, at).astype(BF16)
            if flat:
                out[:, cols_of(at)] = value
            else:
                out[at] = value

        over(4, body)
        return [
            send(out.at[:, cols_of(other)] if flat else out.at[other], landing.at[k], to_z[k])
            for k, other in enumerate(others)
        ]

    def z_sum(pack):
        landing = pack[5]
        total = plane_sum(pack, z)
        for k in range(3):
            total = total + landing[k].astype(F32)
        return total

    i_a = first_hop(io1, far, 0)
    o_a = first_hop(oo1, far, 0)
    i_b = first_hop(io1, n1, 1)
    o_b = first_hop(oo1, n1, 1)
    t_a = first_hop(tt1, far, 0)
    t_b = first_hop(tt1, n1, 1)
    u_a = first_hop(uu1, far, 0)
    u_b = first_hop(uu1, n1, 1)
    p_copy = send(p_ref, p_out, to_z[1])

    arrived([i_a])
    i_2 = second_hop(io1)
    arrived([o_a])
    o_2 = second_hop(oo1)
    arrived([i_b, i_2])
    i_zs = z_hop(io1)
    arrived([o_b, o_2])
    o_zs = z_hop(oo1)
    arrived([t_a])
    t_2 = second_hop(tt1)

    arrived(i_zs)
    i_mine = i_out.at[rows_of(me), cols_of(core * 4 + z)]
    i_out[rows_of(me), cols_of(core * 4 + z)] = z_sum(io1).astype(BF16)
    i_ag = [send(i_mine, i_mine, peer) for peer in to_z]
    arrived(o_zs)
    o_mine = o_out.at[rows_of(me), cols_of(core * 4 + z)]
    o_out[rows_of(me), cols_of(core * 4 + z)] = z_sum(oo1).astype(BF16)
    o_ag = [send(o_mine, o_mine, peer) for peer in to_z]

    def forward(block, peer):
        wide = pl.ds(pl.multiple_of(core * 4 * lanes, 128), 4 * lanes)
        i_part = i_out.at[rows_of(block), wide]
        o_part = o_out.at[rows_of(block), wide]
        return [send(i_part, i_part, peer), send(o_part, o_part, peer)]

    arrived([t_b, t_2])
    t_zs = z_hop(tt1)
    arrived([u_a])
    u_2 = second_hop(uu1)

    arrived(i_ag + o_ag)
    hop1 = forward(me, to_n1)
    hop2 = forward(me, to_n2)
    twin_me = forward(me, to_twin)
    arrived([u_b, u_2])
    u_zs = z_hop(uu1)

    def finish(pack, fin, part):
        total = z_sum(pack)
        fin[0] = total[: total.shape[0] // 2]
        fin[1] = total[total.shape[0] // 2 :]
        wide = fin.shape[2]
        cut = pl.ds(pl.multiple_of((core * 2 + part) * wide, 128), wide)
        t_out[:, cut] = fin[core]
        return send(fin.at[1 - core], t_out.at[:, cut], to_twin)

    arrived(t_zs)
    t_twin = finish(tt1, t_fin, 0)
    arrived(hop1)
    hop3 = forward(n1, to_n2)
    twin_n1 = forward(n1, to_twin)
    arrived(hop2)
    twin_n2 = forward(n2, to_twin)

    arrived(u_zs)
    u_twin = finish(uu1, u_fin, 1)

    arrived(hop3)
    twin_far = forward(far, to_twin)
    arrived([t_twin, u_twin, p_copy] + twin_me + twin_n1 + twin_n2 + twin_far)
    for copy in made:
        copy.wait_send()


def reduce_all(taps, more_taps, inner, outer, pred):
    vmem = pl.BlockSpec(memory_space=pltpu.VMEM)
    t_blk = taps.shape[2:]
    features, wide = inner.shape
    tall, lanes = features // 4, wide // 4
    scratch = []
    for lead in ((2,), (), (), ()):
        flat = pltpu.VMEM(lead + (tall, wide), BF16)
        blocks = pltpu.VMEM(lead + (4,) + t_blk, BF16)
        scratch += [blocks, blocks, flat, flat]
    landing = pltpu.VMEM((3, tall, lanes), BF16)
    blocks = pltpu.VMEM((3,) + t_blk, BF16)
    scratch += [blocks, blocks, landing, landing]
    final = pltpu.VMEM((2, t_blk[0] // 2, t_blk[1]), F32)
    scratch += [final, final, pltpu.SemaphoreType.DMA((48,)), pltpu.SemaphoreType.DMA((48,))]
    return pl.pallas_call(
        reduce_kernel,
        out_shape=(
            jax.ShapeDtypeStruct((t_blk[0] // 2, 4 * t_blk[1]), F32),
            jax.ShapeDtypeStruct((features, 2 * wide), BF16),
            jax.ShapeDtypeStruct((features, 2 * wide), BF16),
            jax.ShapeDtypeStruct(pred.shape, F32),
        ),
        in_specs=[vmem] * 5,
        out_specs=[vmem] * 4,
        scratch_shapes=scratch,
        compiler_params=pltpu.CompilerParams(
            collective_id=0, has_side_effects=True, vmem_limit_bytes=24 * 1024 * 1024
        ),
    )(taps, more_taps, inner, outer, pred)


def on_small_slice(wall_inputs, in_weight, tap_weights, out_weight, cotangent):
    channels = tap_weights.shape[2]
    wide = channels // 2
    rows, features = wall_inputs.shape[1:]
    half = rows // 2
    tm = lax.axis_index("tm")
    shards = lax.axis_size("tm")
    early = tm < shards // 2
    core = tm % 2
    delayed_w, current_w = tap_weights[0, :channels], tap_weights[0, channels:]

    local = jnp.stack([wall_inputs[0], cotangent[0]])
    keep = jnp.where(early, local[:, :half], local[:, half:])
    give = jnp.where(early, local[:, half:], local[:, :half])
    got = lax.ppermute(give, "tm", [(i, (i + shards // 2) % shards) for i in range(shards)])
    low, high = jnp.where(early, keep, got), jnp.where(early, got, keep)
    pairs = jnp.stack([low, high])
    twin = lax.ppermute(pairs, "tm", [(i, i + 1 - 2 * (i % 2)) for i in range(shards)])
    everything = jnp.stack([pairs, twin], axis=1)
    inputs = everything[:, :, 0].reshape(4 * half, features)
    cots = everything[:, :, 1].reshape(4 * half, features)

    hidden = project(inputs, in_weight).astype(BF16)
    lag = hidden[: 2 * half]
    from_lag = project(lag, delayed_w)
    preact = project(hidden, current_w) + jnp.concatenate([jnp.zeros_like(from_lag), from_lag])
    squash = jnp.tanh(preact)
    hidden_1 = (hidden.astype(F32) + squash).astype(BF16)
    own = jnp.concatenate([hidden_1[:half], hidden_1[2 * half : 3 * half]])
    pred = project(own, out_weight)
    upstream = project_back(cots, out_weight)
    pre_grad = (upstream * (1.0 - squash * squash)).astype(BF16)
    late = pre_grad[2 * half :]
    from_late = project_back(late, delayed_w)
    back = upstream + project_back(pre_grad, current_w) + jnp.concatenate(
        [from_late, jnp.zeros_like(from_late)]
    )
    back = back.astype(BF16)

    pre_cols = lax.dynamic_slice_in_dim(pre_grad, core * wide, wide, 1)
    back_cols = lax.dynamic_slice_in_dim(back, core * wide, wide, 1)
    hidden_cols = lax.dynamic_slice_in_dim(hidden_1, core * wide, wide, 1)
    lagged = jnp.concatenate([jnp.zeros_like(lag), lag])
    both = jnp.concatenate([lagged, hidden], axis=1)
    taps, more_taps = [
        contract_rows(both, part).astype(BF16).reshape(4, 4, channels // 8, wide // 2)
        for part in (pre_cols[:, : wide // 2], pre_cols[:, wide // 2 :])
    ]
    inner = contract_rows(inputs, back_cols).astype(BF16)
    outer = contract_rows(cots, hidden_cols).astype(BF16)

    pred_keep = jnp.where(early, pred[:half], pred[half:])
    pred_give = jnp.where(early, pred[half:], pred[:half])
    t_sum, i_sum, o_sum, pred_got = reduce_all(taps, more_taps, inner, outer, pred_give)
    prediction = jnp.concatenate(
        [jnp.where(early, pred_keep, pred_got), jnp.where(early, pred_got, pred_keep)]
    )[None]
    grad_taps = t_sum[None]
    grad_in = i_sum.astype(F32)
    grad_out = o_sum.astype(F32).T
    return prediction, grad_in, grad_taps, grad_out


def solution(mesh):
    in_specs = (P("dp", "tm", None), P(), P(), P(), P("dp", "tm", None))
    out_specs = (P("dp", "tm", None), P(), P(None, ("dp", "tm"), None), P())
    small = mesh.shape["dp"] == 4 and mesh.shape["tm"] == 8
    return jax.shard_map(
        on_small_slice if small else on_device,
        mesh=mesh, in_specs=in_specs, out_specs=out_specs, check_vma=False,
    )
```

```python
import jax
import jax.numpy as jnp
from jax import lax
from jax.experimental import pallas as pl
from jax.experimental.pallas import tpu as pltpu
from jax.sharding import PartitionSpec as P

LAYERS = 1
DILATION = 512


def from_behind(x, axis, by):
    size = lax.axis_size(axis)
    pairs = [(i, i + by) for i in range(size) if 0 <= i + by < size]
    return lax.ppermute(x, axis, pairs)


def project(left, weight):
    rows = left.reshape(-1, left.shape[-1])
    return jnp.dot(rows, weight, preferred_element_type=jnp.float32).reshape(
        left.shape[:-1] + (weight.shape[-1],)
    )


def project_back(left, weight):
    rows = left.reshape(-1, left.shape[-1])
    step_outcome = lax.dot_general(
        rows, weight, (((1,), (1,)), ((), ())), preferred_element_type=jnp.float32
    )
    return step_outcome.reshape(left.shape[:-1] + (weight.shape[0],))


def contract_rows(left, right):
    return lax.dot_general(
        left.reshape(-1, left.shape[-1]),
        right.reshape(-1, right.shape[-1]),
        (((0,), (0,)), ((), ())),
        preferred_element_type=jnp.float32,
    )


def lag_rows(hidden, dilation):
    shard_len = hidden.shape[1]
    whole_shards, remainder = divmod(dilation, shard_len)
    head_rows = hidden
    head_rows = from_behind(head_rows, "tm", whole_shards)
    return head_rows


def lead_sums(values, dilation):
    shard_len = values.shape[1]
    whole_shards, remainder = divmod(dilation, shard_len)
    head_rows = values
    head_rows = from_behind(head_rows.astype(jnp.bfloat16), "tm", -whole_shards).astype(
        head_rows.dtype
    )
    return head_rows


def reduce_taps(partial_value):
    per_member_split = lax.psum_scatter(partial_value, "dp", scatter_dimension=0, tiled=True)
    return lax.psum_scatter(per_member_split, "tm", scatter_dimension=0, tiled=True)


def on_device(wall_inputs, in_weight, tap_weights, out_weight, cotangent):
    channels = tap_weights.shape[2]
    hidden = project(wall_inputs, in_weight).astype(jnp.bfloat16)
    layer_at = 0
    lagged = lag_rows(hidden, DILATION)
    preact = project(lagged, tap_weights[layer_at, :channels]) + project(
        hidden, tap_weights[layer_at, channels:]
    )
    activation_function = jnp.tanh(preact)
    stored = [(lagged, hidden, activation_function)]
    hidden = (hidden.astype(jnp.float32) + activation_function).astype(jnp.bfloat16)
    prediction = project(hidden, out_weight)
    grad_out = lax.psum(contract_rows(hidden, cotangent), ("dp", "tm"))
    upstream = project_back(cotangent, out_weight)
    filter_tap_gradient = [None] * LAYERS
    for layer_at in reversed(range(LAYERS)):
        lagged, before, activation_function = stored[layer_at]
        pre_grad = (upstream * (1.0 - activation_function * activation_function)).astype(
            jnp.bfloat16
        )
        partial_value = jnp.concatenate(
            [contract_rows(lagged, pre_grad), contract_rows(before, pre_grad)], axis=0
        )
        filter_tap_gradient[layer_at] = reduce_taps(partial_value)
        direct = project_back(pre_grad, tap_weights[layer_at, channels:])
        delayed = lead_sums(project_back(pre_grad, tap_weights[layer_at, :channels]), DILATION)
        upstream = upstream + direct + delayed
    back_zero = upstream.astype(jnp.bfloat16)
    grad_in = lax.psum(contract_rows(wall_inputs, back_zero), ("dp", "tm"))
    return (prediction, grad_in, jnp.stack(filter_tap_gradient), grad_out)


BF16 = jnp.bfloat16
F32 = jnp.float32


def reduce_kernel(
    t_ref, u_ref, i_ref, o_ref, p_ref,
    t_out, i_out, o_out, p_out,
    t_r1, u_r1, i_r1, o_r1, t_s2, u_s2, i_s2, o_s2, t_r2, u_r2, i_r2, o_r2,
    t_z, u_z, i_z, o_z, t_rz, u_rz, i_rz, o_rz, t_fin, u_fin, p_buf,
    send_sems, recv_sems,
):
    me = lax.axis_index("dp")
    tm = lax.axis_index("tm")
    z, core = tm // 2, tm % 2
    x_peer = me + 1 - 2 * (me % 2)
    y_peer = me + 2 - 4 * (me // 2)
    n1 = x_peer * (1 - core) + y_peer * core
    n2 = y_peer * (1 - core) + x_peer * core
    far = 3 - me
    others = [z + 1 - 2 * (z % 2), (z + 2) % 4, 3 - z]
    twin = z * 2 + 1 - core

    to_n1 = {"dp": n1, "tm": tm}
    to_n2 = {"dp": n2, "tm": tm}
    to_z = [{"dp": me, "tm": other * 2 + core} for other in others]
    to_twin = {"dp": me, "tm": twin}

    barrier = pltpu.get_barrier_semaphore()
    peers = [to_n1, to_n2, to_twin] + to_z
    for peer in peers:
        pl.semaphore_signal(barrier, inc=1, device_id=peer, device_id_type=pl.DeviceIdType.MESH)
    pl.semaphore_wait(barrier, len(peers))

    made = []

    def send(src, dst, peer):
        at = len(made)
        copy = pltpu.make_async_remote_copy(
            src_ref=src, dst_ref=dst, send_sem=send_sems.at[at], recv_sem=recv_sems.at[at],
            device_id=peer, device_id_type=pl.DeviceIdType.MESH,
        )
        copy.start()
        made.append(copy)
        return copy

    def arrived(copies):
        for copy in copies:
            copy.wait_recv()

    def over(count, body):
        def step(at, carry):
            body(at)
            return carry

        lax.fori_loop(0, count, step, 0)

    io1 = (i_ref, i_r1, i_s2, i_r2, i_z, i_rz)
    oo1 = (o_ref, o_r1, o_s2, o_r2, o_z, o_rz)
    tt1 = (t_ref, t_r1, t_s2, t_r2, t_z, t_rz)
    uu1 = (u_ref, u_r1, u_s2, u_r2, u_z, u_rz)
    tall = i_s2.shape[0]
    lanes = i_rz.shape[2]

    def rows_of(block):
        return pl.ds(pl.multiple_of(block * tall, 16), tall)

    def cols_of(at):
        return pl.ds(pl.multiple_of(at * lanes, 128), lanes)

    def first_hop(pack, block, slot):
        flat = len(pack[0].shape) == 2
        src = pack[0].at[rows_of(block)] if flat else pack[0].at[block]
        return send(src, pack[1].at[slot], to_n1)

    def second_hop(pack):
        local, r1, s2, r2 = pack[:4]

        def body(at):
            if len(local.shape) == 2:
                cut = cols_of(at)
                mine = local[rows_of(n2), cut].astype(F32)
                s2[:, cut] = (mine + r1[0, :, cut].astype(F32)).astype(BF16)
            else:
                s2[at] = (local[n2, at].astype(F32) + r1[0, at].astype(F32)).astype(BF16)

        over(4, body)
        return send(s2, r2, to_n2)

    def plane_sum(pack, at):
        local, r1, _, r2 = pack[:4]
        if len(local.shape) == 2:
            cut = cols_of(at)
            mine, first, second = local[rows_of(me), cut], r1[1, :, cut], r2[:, cut]
        else:
            mine, first, second = local[me, at], r1[1, at], r2[at]
        return mine.astype(F32) + first.astype(F32) + second.astype(F32)

    def z_hop(pack):
        out, landing = pack[4], pack[5]
        flat = len(out.shape) == 2

        def body(at):
            value = plane_sum(pack, at).astype(BF16)
            if flat:
                out[:, cols_of(at)] = value
            else:
                out[at] = value

        over(4, body)
        return [
            send(out.at[:, cols_of(other)] if flat else out.at[other], landing.at[k], to_z[k])
            for k, other in enumerate(others)
        ]

    def z_sum(pack):
        landing = pack[5]
        total = plane_sum(pack, z)
        for k in range(3):
            total = total + landing[k].astype(F32)
        return total

    i_a = first_hop(io1, far, 0)
    o_a = first_hop(oo1, far, 0)
    i_b = first_hop(io1, n1, 1)
    o_b = first_hop(oo1, n1, 1)
    t_a = first_hop(tt1, far, 0)
    t_b = first_hop(tt1, n1, 1)
    u_a = first_hop(uu1, far, 0)
    u_b = first_hop(uu1, n1, 1)
    half = p_ref.shape[0] // 2
    late = tm // 4
    kept = pl.ds(pl.multiple_of(late * half, 8), half)
    given = pl.ds(pl.multiple_of((1 - late) * half, 8), half)
    p_copy = send(p_ref.at[given], p_buf.at[kept], to_z[1])
    p_buf[kept] = p_ref[kept]

    arrived([i_a])
    i_2 = second_hop(io1)
    arrived([o_a])
    o_2 = second_hop(oo1)
    arrived([i_b, i_2])
    i_zs = z_hop(io1)
    arrived([o_b, o_2])
    o_zs = z_hop(oo1)
    arrived([t_a])
    t_2 = second_hop(tt1)

    arrived(i_zs)
    i_mine = i_out.at[rows_of(me), cols_of(core * 4 + z)]
    i_out[rows_of(me), cols_of(core * 4 + z)] = z_sum(io1).astype(BF16)
    i_ag = [send(i_mine, i_mine, peer) for peer in to_z]
    arrived(o_zs)
    o_mine = o_out.at[rows_of(me), cols_of(core * 4 + z)]
    o_out[rows_of(me), cols_of(core * 4 + z)] = z_sum(oo1).astype(BF16)
    o_ag = [send(o_mine, o_mine, peer) for peer in to_z]

    def forward(block, peer):
        wide = pl.ds(pl.multiple_of(core * 4 * lanes, 128), 4 * lanes)
        i_part = i_out.at[rows_of(block), wide]
        o_part = o_out.at[rows_of(block), wide]
        return [send(i_part, i_part, peer), send(o_part, o_part, peer)]

    arrived([t_b, t_2])
    t_zs = z_hop(tt1)
    arrived([u_a])
    u_2 = second_hop(uu1)

    arrived(i_ag + o_ag)
    hop1 = forward(me, to_n1)
    hop2 = forward(me, to_n2)
    twin_me = forward(me, to_twin)
    arrived([u_b, u_2])
    u_zs = z_hop(uu1)

    def finish(pack, fin, part):
        total = z_sum(pack)
        fin[0] = total[: total.shape[0] // 2]
        fin[1] = total[total.shape[0] // 2 :]
        wide = fin.shape[2]
        cut = pl.ds(pl.multiple_of((core * 2 + part) * wide, 128), wide)
        t_out[:, cut] = fin[core]
        return send(fin.at[1 - core], t_out.at[:, cut], to_twin)

    arrived([p_copy])
    p_out[...] = p_buf[...].T

    arrived(t_zs)
    t_twin = finish(tt1, t_fin, 0)
    arrived(hop1)
    hop3 = forward(n1, to_n2)
    twin_n1 = forward(n1, to_twin)
    arrived(hop2)
    twin_n2 = forward(n2, to_twin)

    arrived(u_zs)
    u_twin = finish(uu1, u_fin, 1)

    arrived(hop3)
    twin_far = forward(far, to_twin)
    arrived([t_twin, u_twin] + twin_me + twin_n1 + twin_n2 + twin_far)
    for copy in made:
        copy.wait_send()


def reduce_all(taps, more_taps, inner, outer, pred):
    vmem = pl.BlockSpec(memory_space=pltpu.VMEM)
    t_blk = taps.shape[2:]
    features, wide = inner.shape
    tall, lanes = features // 4, wide // 4
    scratch = []
    for lead in ((2,), (), (), ()):
        flat = pltpu.VMEM(lead + (tall, wide), BF16)
        blocks = pltpu.VMEM(lead + (4,) + t_blk, BF16)
        scratch += [blocks, blocks, flat, flat]
    landing = pltpu.VMEM((3, tall, lanes), BF16)
    blocks = pltpu.VMEM((3,) + t_blk, BF16)
    scratch += [blocks, blocks, landing, landing]
    final = pltpu.VMEM((2, t_blk[0] // 2, t_blk[1]), F32)
    scratch += [final, final, pltpu.VMEM(pred.shape, F32)]
    scratch += [pltpu.SemaphoreType.DMA((48,)), pltpu.SemaphoreType.DMA((48,))]
    return pl.pallas_call(
        reduce_kernel,
        out_shape=(
            jax.ShapeDtypeStruct((t_blk[0] // 2, 4 * t_blk[1]), F32),
            jax.ShapeDtypeStruct((features, 2 * wide), BF16),
            jax.ShapeDtypeStruct((features, 2 * wide), BF16),
            jax.ShapeDtypeStruct(pred.shape[::-1], F32),
        ),
        in_specs=[vmem] * 5,
        out_specs=[vmem] * 4,
        scratch_shapes=scratch,
        compiler_params=pltpu.CompilerParams(
            collective_id=0, has_side_effects=True, vmem_limit_bytes=24 * 1024 * 1024
        ),
    )(taps, more_taps, inner, outer, pred)


def pair_kernel(x_ref, c_ref, x_out, c_out, send_sems, recv_sems):
    me = lax.axis_index("dp")
    tm = lax.axis_index("tm")
    z, core = tm // 2, tm % 2
    late = tm // 4
    mesh_ids = pl.DeviceIdType.MESH
    peer = {"dp": me, "tm": ((z + 2) % 4) * 2 + core}
    twin = {"dp": me, "tm": z * 2 + 1 - core}
    half = x_ref.shape[0] // 2

    def cut(at):
        return pl.ds(pl.multiple_of(at * half, 16), half)

    barrier = pltpu.get_barrier_semaphore()
    for other in (peer, twin):
        pl.semaphore_signal(barrier, inc=1, device_id=other, device_id_type=mesh_ids)
    pl.semaphore_wait(barrier, 2)

    def send(at, src, dst, to):
        copy = pltpu.make_async_remote_copy(
            src_ref=src, dst_ref=dst, send_sem=send_sems.at[at], recv_sem=recv_sems.at[at],
            device_id=to, device_id_type=mesh_ids,
        )
        copy.start()
        return copy

    pairs = ((x_ref, x_out), (c_ref, c_out))
    far = [
        send(k, src.at[cut(1 - late)], out.at[cut(2 * late)], peer)
        for k, (src, out) in enumerate(pairs)
    ]
    near = [
        send(2 + k, src.at[cut(late)], out.at[cut(2 * late + 1)], twin)
        for k, (src, out) in enumerate(pairs)
    ]
    for src, out in pairs:
        out[cut(2 * late)] = src[cut(late)]
    for k, (_, out) in enumerate(pairs):
        far[k].wait_recv()
        got = 2 * (1 - late)
        near.append(send(4 + k, out.at[cut(got)], out.at[cut(got + 1)], twin))
    for copy in near:
        copy.wait_recv()
    for copy in far + near:
        copy.wait_send()


def pair_rows(x, c):
    vmem = pl.BlockSpec(memory_space=pltpu.VMEM)
    rows, features = x.shape
    return pl.pallas_call(
        pair_kernel,
        out_shape=(jax.ShapeDtypeStruct((2 * rows, features), BF16),) * 2,
        in_specs=[vmem] * 2,
        out_specs=[vmem] * 2,
        scratch_shapes=[pltpu.SemaphoreType.DMA((6,)), pltpu.SemaphoreType.DMA((6,))],
        compiler_params=pltpu.CompilerParams(
            collective_id=1, has_side_effects=True, vmem_limit_bytes=8 * 1024 * 1024
        ),
    )(x, c)


def on_small_slice(wall_inputs, in_weight, tap_weights, out_weight, cotangent):
    channels = tap_weights.shape[2]
    wide = channels // 2
    rows, features = wall_inputs.shape[1:]
    half = rows // 2
    tm = lax.axis_index("tm")
    core = tm % 2
    delayed_w, current_w = tap_weights[0, :channels], tap_weights[0, channels:]

    inputs, cots = pair_rows(wall_inputs[0], cotangent[0])

    hidden = project(inputs, in_weight).astype(BF16)
    lag = hidden[: 2 * half]
    from_lag = project(lag, delayed_w)
    preact = project(hidden, current_w) + jnp.concatenate([jnp.zeros_like(from_lag), from_lag])
    squash = jnp.tanh(preact)
    hidden_1 = (hidden.astype(F32) + squash).astype(BF16)
    own = jnp.concatenate([hidden_1[:half], hidden_1[2 * half : 3 * half]])
    pred = project(own, out_weight)
    upstream = project_back(cots, out_weight)
    pre_grad = (upstream * (1.0 - squash * squash)).astype(BF16)
    late = pre_grad[2 * half :]
    from_late = project_back(late, delayed_w)
    back = upstream + project_back(pre_grad, current_w) + jnp.concatenate(
        [from_late, jnp.zeros_like(from_late)]
    )
    back = back.astype(BF16)

    pre_cols = lax.dynamic_slice_in_dim(pre_grad, core * wide, wide, 1)
    back_cols = lax.dynamic_slice_in_dim(back, core * wide, wide, 1)
    hidden_cols = lax.dynamic_slice_in_dim(hidden_1, core * wide, wide, 1)
    lagged = jnp.concatenate([jnp.zeros_like(lag), lag])
    both = jnp.concatenate([lagged, hidden], axis=1)
    taps, more_taps = [
        contract_rows(both, part).astype(BF16).reshape(4, 4, channels // 8, wide // 2)
        for part in (pre_cols[:, : wide // 2], pre_cols[:, wide // 2 :])
    ]
    inner = contract_rows(inputs, back_cols).astype(BF16)
    outer = contract_rows(cots, hidden_cols).astype(BF16)

    t_sum, i_sum, o_sum, pred_sum = reduce_all(taps, more_taps, inner, outer, pred)
    prediction = pred_sum.T[None]
    grad_taps = t_sum[None]
    grad_in = i_sum.astype(F32)
    grad_out = o_sum.astype(F32).T
    return prediction, grad_in, grad_taps, grad_out


def solution(mesh):
    in_specs = (P("dp", "tm", None), P(), P(), P(), P("dp", "tm", None))
    out_specs = (P("dp", "tm", None), P(), P(None, ("dp", "tm"), None), P())
    small = mesh.shape["dp"] == 4 and mesh.shape["tm"] == 8
    return jax.shard_map(
        on_small_slice if small else on_device,
        mesh=mesh, in_specs=in_specs, out_specs=out_specs, check_vma=False,
    )
```

```python
import jax
import jax.numpy as jnp
from jax import lax
from jax.experimental import pallas as pl
from jax.experimental.pallas import tpu as pltpu
from jax.sharding import PartitionSpec as P

LAYERS = 1
DILATION = 512


def from_behind(x, axis, by):
    size = lax.axis_size(axis)
    pairs = [(i, i + by) for i in range(size) if 0 <= i + by < size]
    return lax.ppermute(x, axis, pairs)


def project(left, weight):
    rows = left.reshape(-1, left.shape[-1])
    return jnp.dot(rows, weight, preferred_element_type=jnp.float32).reshape(
        left.shape[:-1] + (weight.shape[-1],)
    )


def project_back(left, weight):
    rows = left.reshape(-1, left.shape[-1])
    step_outcome = lax.dot_general(
        rows, weight, (((1,), (1,)), ((), ())), preferred_element_type=jnp.float32
    )
    return step_outcome.reshape(left.shape[:-1] + (weight.shape[0],))


def contract_rows(left, right):
    return lax.dot_general(
        left.reshape(-1, left.shape[-1]),
        right.reshape(-1, right.shape[-1]),
        (((0,), (0,)), ((), ())),
        preferred_element_type=jnp.float32,
    )


def lag_rows(hidden, dilation):
    shard_len = hidden.shape[1]
    whole_shards, remainder = divmod(dilation, shard_len)
    head_rows = hidden
    head_rows = from_behind(head_rows, "tm", whole_shards)
    return head_rows


def lead_sums(values, dilation):
    shard_len = values.shape[1]
    whole_shards, remainder = divmod(dilation, shard_len)
    head_rows = values
    head_rows = from_behind(head_rows.astype(jnp.bfloat16), "tm", -whole_shards).astype(
        head_rows.dtype
    )
    return head_rows


def reduce_taps(partial_value):
    per_member_split = lax.psum_scatter(partial_value, "dp", scatter_dimension=0, tiled=True)
    return lax.psum_scatter(per_member_split, "tm", scatter_dimension=0, tiled=True)


def on_device(wall_inputs, in_weight, tap_weights, out_weight, cotangent):
    channels = tap_weights.shape[2]
    hidden = project(wall_inputs, in_weight).astype(jnp.bfloat16)
    layer_at = 0
    lagged = lag_rows(hidden, DILATION)
    preact = project(lagged, tap_weights[layer_at, :channels]) + project(
        hidden, tap_weights[layer_at, channels:]
    )
    activation_function = jnp.tanh(preact)
    stored = [(lagged, hidden, activation_function)]
    hidden = (hidden.astype(jnp.float32) + activation_function).astype(jnp.bfloat16)
    prediction = project(hidden, out_weight)
    grad_out = lax.psum(contract_rows(hidden, cotangent), ("dp", "tm"))
    upstream = project_back(cotangent, out_weight)
    filter_tap_gradient = [None] * LAYERS
    for layer_at in reversed(range(LAYERS)):
        lagged, before, activation_function = stored[layer_at]
        pre_grad = (upstream * (1.0 - activation_function * activation_function)).astype(
            jnp.bfloat16
        )
        partial_value = jnp.concatenate(
            [contract_rows(lagged, pre_grad), contract_rows(before, pre_grad)], axis=0
        )
        filter_tap_gradient[layer_at] = reduce_taps(partial_value)
        direct = project_back(pre_grad, tap_weights[layer_at, channels:])
        delayed = lead_sums(project_back(pre_grad, tap_weights[layer_at, :channels]), DILATION)
        upstream = upstream + direct + delayed
    back_zero = upstream.astype(jnp.bfloat16)
    grad_in = lax.psum(contract_rows(wall_inputs, back_zero), ("dp", "tm"))
    return (prediction, grad_in, jnp.stack(filter_tap_gradient), grad_out)


BF16 = jnp.bfloat16
F32 = jnp.float32


def reduce_kernel(
    t_ref, u_ref, i_ref, o_ref, p_ref,
    t_out, i_out, o_out, p_out,
    t_r1, u_r1, i_r1, o_r1, t_s2, u_s2, i_s2, o_s2, t_r2, u_r2, i_r2, o_r2,
    t_z, u_z, i_z, o_z, t_rz, u_rz, i_rz, o_rz, t_fin, u_fin, p_buf,
    send_sems, recv_sems,
):
    me = lax.axis_index("dp")
    tm = lax.axis_index("tm")
    z, core = tm // 2, tm % 2
    x_peer = me + 1 - 2 * (me % 2)
    y_peer = me + 2 - 4 * (me // 2)
    n1 = x_peer * (1 - core) + y_peer * core
    n2 = y_peer * (1 - core) + x_peer * core
    far = 3 - me
    others = [z + 1 - 2 * (z % 2), (z + 2) % 4, 3 - z]
    twin = z * 2 + 1 - core

    to_n1 = {"dp": n1, "tm": tm}
    to_n2 = {"dp": n2, "tm": tm}
    to_z = [{"dp": me, "tm": other * 2 + core} for other in others]
    to_twin = {"dp": me, "tm": twin}

    barrier = pltpu.get_barrier_semaphore()
    peers = [to_n1, to_n2, to_twin] + to_z
    for peer in peers:
        pl.semaphore_signal(barrier, inc=1, device_id=peer, device_id_type=pl.DeviceIdType.MESH)
    pl.semaphore_wait(barrier, len(peers))

    made = []

    def send(src, dst, peer):
        at = len(made)
        copy = pltpu.make_async_remote_copy(
            src_ref=src, dst_ref=dst, send_sem=send_sems.at[at], recv_sem=recv_sems.at[at],
            device_id=peer, device_id_type=pl.DeviceIdType.MESH,
        )
        copy.start()
        made.append(copy)
        return copy

    def arrived(copies):
        for copy in copies:
            copy.wait_recv()

    def over(count, body):
        def step(at, carry):
            body(at)
            return carry

        lax.fori_loop(0, count, step, 0)

    io1 = (i_ref, i_r1, i_s2, i_r2, i_z, i_rz)
    oo1 = (o_ref, o_r1, o_s2, o_r2, o_z, o_rz)
    tt1 = (t_ref, t_r1, t_s2, t_r2, t_z, t_rz)
    uu1 = (u_ref, u_r1, u_s2, u_r2, u_z, u_rz)
    tall = i_s2.shape[0]
    lanes = i_rz.shape[2]

    def rows_of(block):
        return pl.ds(pl.multiple_of(block * tall, 16), tall)

    def cols_of(at):
        return pl.ds(pl.multiple_of(at * lanes, 128), lanes)

    def first_hop(pack, block, slot):
        flat = len(pack[0].shape) == 2
        src = pack[0].at[rows_of(block)] if flat else pack[0].at[block]
        return send(src, pack[1].at[slot], to_n1)

    def second_hop(pack):
        local, r1, s2, r2 = pack[:4]

        def body(at):
            if len(local.shape) == 2:
                cut = cols_of(at)
                mine = local[rows_of(n2), cut].astype(F32)
                s2[:, cut] = (mine + r1[0, :, cut].astype(F32)).astype(BF16)
            else:
                s2[at] = (local[n2, at].astype(F32) + r1[0, at].astype(F32)).astype(BF16)

        over(4, body)
        return send(s2, r2, to_n2)

    def plane_sum(pack, at):
        local, r1, _, r2 = pack[:4]
        if len(local.shape) == 2:
            cut = cols_of(at)
            mine, first, second = local[rows_of(me), cut], r1[1, :, cut], r2[:, cut]
        else:
            mine, first, second = local[me, at], r1[1, at], r2[at]
        return mine.astype(F32) + first.astype(F32) + second.astype(F32)

    def z_hop(pack):
        out, landing = pack[4], pack[5]
        flat = len(out.shape) == 2

        def body(at):
            value = plane_sum(pack, at).astype(BF16)
            if flat:
                out[:, cols_of(at)] = value
            else:
                out[at] = value

        over(4, body)
        return [
            send(out.at[:, cols_of(other)] if flat else out.at[other], landing.at[k], to_z[k])
            for k, other in enumerate(others)
        ]

    def z_sum(pack):
        landing = pack[5]
        total = plane_sum(pack, z)
        for k in range(3):
            total = total + landing[k].astype(F32)
        return total

    i_a = first_hop(io1, far, 0)
    o_a = first_hop(oo1, far, 0)
    i_b = first_hop(io1, n1, 1)
    o_b = first_hop(oo1, n1, 1)
    t_a = first_hop(tt1, far, 0)
    t_b = first_hop(tt1, n1, 1)
    u_a = first_hop(uu1, far, 0)
    u_b = first_hop(uu1, n1, 1)
    half = p_ref.shape[0] // 2
    late = tm // 4
    kept = pl.ds(pl.multiple_of(late * half, 8), half)
    given = pl.ds(pl.multiple_of((1 - late) * half, 8), half)
    p_copy = send(p_ref.at[given], p_buf.at[kept], to_z[1])
    p_buf[kept] = p_ref[kept]

    arrived([i_a])
    i_2 = second_hop(io1)
    arrived([o_a])
    o_2 = second_hop(oo1)
    arrived([i_b, i_2])
    i_zs = z_hop(io1)
    arrived([o_b, o_2])
    o_zs = z_hop(oo1)
    arrived([t_a])
    t_2 = second_hop(tt1)

    arrived(i_zs)
    i_mine = i_out.at[rows_of(me), cols_of(core * 4 + z)]
    i_out[rows_of(me), cols_of(core * 4 + z)] = z_sum(io1).astype(BF16)
    i_ag = [send(i_mine, i_mine, peer) for peer in to_z]
    arrived(o_zs)
    o_mine = o_out.at[rows_of(me), cols_of(core * 4 + z)]
    o_out[rows_of(me), cols_of(core * 4 + z)] = z_sum(oo1).astype(BF16)
    o_ag = [send(o_mine, o_mine, peer) for peer in to_z]

    def forward(block, peer):
        wide = pl.ds(pl.multiple_of(core * 4 * lanes, 128), 4 * lanes)
        i_part = i_out.at[rows_of(block), wide]
        o_part = o_out.at[rows_of(block), wide]
        return [send(i_part, i_part, peer), send(o_part, o_part, peer)]

    arrived([t_b, t_2])
    t_zs = z_hop(tt1)
    arrived([u_a])
    u_2 = second_hop(uu1)

    arrived(i_ag + o_ag)
    hop1 = forward(me, to_n1)
    hop2 = forward(me, to_n2)
    twin_me = forward(me, to_twin)
    arrived([u_b, u_2])
    u_zs = z_hop(uu1)

    def finish(pack, fin, part):
        total = z_sum(pack)
        fin[0] = total[: total.shape[0] // 2]
        fin[1] = total[total.shape[0] // 2 :]
        wide = fin.shape[2]
        cut = pl.ds(pl.multiple_of((core * 2 + part) * wide, 128), wide)
        t_out[:, cut] = fin[core]
        return send(fin.at[1 - core], t_out.at[:, cut], to_twin)

    arrived([p_copy])
    p_out[...] = p_buf[...].T

    arrived(t_zs)
    t_twin = finish(tt1, t_fin, 0)
    arrived(hop1)
    hop3 = forward(n1, to_n2)
    twin_n1 = forward(n1, to_twin)
    arrived(hop2)
    twin_n2 = forward(n2, to_twin)

    arrived(u_zs)
    u_twin = finish(uu1, u_fin, 1)

    arrived(hop3)
    twin_far = forward(far, to_twin)
    arrived([t_twin, u_twin] + twin_me + twin_n1 + twin_n2 + twin_far)
    for copy in made:
        copy.wait_send()


def reduce_all(taps, more_taps, inner, outer, pred):
    vmem = pl.BlockSpec(memory_space=pltpu.VMEM)
    t_blk = taps.shape[2:]
    features, wide = inner.shape
    tall, lanes = features // 4, wide // 4
    scratch = []
    for lead in ((2,), (), (), ()):
        flat = pltpu.VMEM(lead + (tall, wide), BF16)
        blocks = pltpu.VMEM(lead + (4,) + t_blk, BF16)
        scratch += [blocks, blocks, flat, flat]
    landing = pltpu.VMEM((3, tall, lanes), BF16)
    blocks = pltpu.VMEM((3,) + t_blk, BF16)
    scratch += [blocks, blocks, landing, landing]
    final = pltpu.VMEM((2, t_blk[0] // 2, t_blk[1]), F32)
    scratch += [final, final, pltpu.VMEM(pred.shape, F32)]
    scratch += [pltpu.SemaphoreType.DMA((48,)), pltpu.SemaphoreType.DMA((48,))]
    return pl.pallas_call(
        reduce_kernel,
        out_shape=(
            jax.ShapeDtypeStruct((t_blk[0] // 2, 4 * t_blk[1]), F32),
            jax.ShapeDtypeStruct((features, 2 * wide), BF16),
            jax.ShapeDtypeStruct((features, 2 * wide), BF16),
            jax.ShapeDtypeStruct(pred.shape[::-1], F32),
        ),
        in_specs=[vmem] * 5,
        out_specs=[vmem] * 4,
        scratch_shapes=scratch,
        compiler_params=pltpu.CompilerParams(
            collective_id=0, has_side_effects=True, vmem_limit_bytes=24 * 1024 * 1024
        ),
    )(taps, more_taps, inner, outer, pred)


def on_small_slice(wall_inputs, in_weight, tap_weights, out_weight, cotangent):
    channels = tap_weights.shape[2]
    wide = channels // 2
    rows, features = wall_inputs.shape[1:]
    half = rows // 2
    tm = lax.axis_index("tm")
    shards = lax.axis_size("tm")
    early = tm < shards // 2
    core = tm % 2
    delayed_w, current_w = tap_weights[0, :channels], tap_weights[0, channels:]

    local = jnp.stack([wall_inputs[0], cotangent[0]])
    keep = jnp.where(early, local[:, :half], local[:, half:])
    give = jnp.where(early, local[:, half:], local[:, :half])
    got = lax.ppermute(give, "tm", [(i, (i + shards // 2) % shards) for i in range(shards)])
    low, high = jnp.where(early, keep, got), jnp.where(early, got, keep)
    pairs = jnp.stack([low, high])
    twin = lax.ppermute(pairs, "tm", [(i, i + 1 - 2 * (i % 2)) for i in range(shards)])
    everything = jnp.stack([pairs, twin], axis=1)
    inputs = everything[:, :, 0].reshape(4 * half, features)
    cots = everything[:, :, 1].reshape(4 * half, features)

    hidden = project(inputs, in_weight).astype(BF16)
    lag = hidden[: 2 * half]
    from_lag = project(lag, delayed_w)
    preact = project(hidden, current_w) + jnp.concatenate([jnp.zeros_like(from_lag), from_lag])
    squash = jnp.tanh(preact)
    hidden_1 = (hidden.astype(F32) + squash).astype(BF16)
    own = jnp.concatenate([hidden_1[:half], hidden_1[2 * half : 3 * half]])
    pred = project(own, out_weight)
    upstream = project_back(cots, out_weight)
    pre_grad = (upstream * (1.0 - squash * squash)).astype(BF16)
    late = pre_grad[2 * half :]
    from_late = project_back(late, delayed_w)
    back = upstream + project_back(pre_grad, current_w) + jnp.concatenate(
        [from_late, jnp.zeros_like(from_late)]
    )
    back = back.astype(BF16)

    pre_cols = lax.dynamic_slice_in_dim(pre_grad, core * wide, wide, 1)
    back_cols = lax.dynamic_slice_in_dim(back, core * wide, wide, 1)
    hidden_cols = lax.dynamic_slice_in_dim(hidden_1, core * wide, wide, 1)
    lagged = jnp.concatenate([jnp.zeros_like(lag), lag])
    both = jnp.concatenate([lagged, hidden], axis=1)
    taps, more_taps = [
        contract_rows(both, part).astype(BF16).reshape(4, 4, channels // 8, wide // 2)
        for part in (pre_cols[:, : wide // 2], pre_cols[:, wide // 2 :])
    ]
    inner = contract_rows(inputs, back_cols).astype(BF16)
    outer = contract_rows(cots, hidden_cols).astype(BF16)

    t_sum, i_sum, o_sum, pred_sum = reduce_all(taps, more_taps, inner, outer, pred)
    prediction = pred_sum.T[None]
    grad_taps = t_sum[None]
    grad_in = i_sum.astype(F32)
    grad_out = o_sum.astype(F32).T
    return prediction, grad_in, grad_taps, grad_out


def solution(mesh):
    in_specs = (P("dp", "tm", None), P(), P(), P(), P("dp", "tm", None))
    out_specs = (P("dp", "tm", None), P(), P(None, ("dp", "tm"), None), P())
    small = mesh.shape["dp"] == 4 and mesh.shape["tm"] == 8
    return jax.shard_map(
        on_small_slice if small else on_device,
        mesh=mesh, in_specs=in_specs, out_specs=out_specs, check_vma=False,
    )
```
